32 devices in a mesh: seq: 16 (over z, x, core), dp: 2 (over y).
Axes of the slice: x: 2, y: 2, z: 4, core: 2. Of those that a mesh axis runs over, the one named last changes fastest.
Arguments:
- queries: bfloat16 [2, 1024, 2048], P(None, 'seq', 'dp'), may hold values from -10 to 10
- key_rows: bfloat16 [2, 1024, 2048], P(None, 'seq', 'dp'), may hold values from -10 to 10
- value_rows: bfloat16 [2, 1024, 2048], P(None, 'seq', 'dp'), may hold values from -6 to 6
- query_tangent: bfloat16 [2, 1024, 2048], P(None, 'seq', 'dp'), may hold values from -6 to 6
- key_tangent: bfloat16 [2, 1024, 2048], P(None, 'seq', 'dp'), may hold values from -6 to 6
- out_adjoint: bfloat16 [2, 1024, 2048], P(None, 'seq', 'dp'), may hold values from -6 to 6
Outputs:
- query_product: bfloat16 [2, 1024, 2048], P(None, 'seq', 'dp')
- key_product: bfloat16 [2, 1024, 2048], P(None, 'seq', 'dp')
- value_product: bfloat16 [2, 1024, 2048], P(None, 'seq', 'dp')
- curvature: float32 [2, 16], replicated
The draws below stay inside these ranges and needn't reach their ends.
All inputs are finite; a program needn't handle non-finite values.
Results may differ from the reference program's by a relative error of at most 0.0051.
Values may be sent and summed in bfloat16 or wider, within the bound.
A program may use at most 64 MiB of HBM per device.

```python
import jax
import jax.numpy as jnp
from jax import lax

HEAD_DIM = 128
SEQUENCE_TOKENS = 1024
HEADS = 16
BATCH_SEQUENCES = 2


def draw_pair(key):
    root_random_key = jax.random.fold_in(key, 7)
    random_key_for_query, random_key_for_keys = jax.random.split(root_random_key, 2)
    shape = (BATCH_SEQUENCES, SEQUENCE_TOKENS, HEADS * HEAD_DIM)
    query_draw = jax.random.normal(random_key_for_query, shape, jnp.float32)
    keys_draw = jax.random.normal(random_key_for_keys, shape, jnp.float32)
    query_draw = jnp.clip(query_draw, -10.0, 10.0)
    keys_draw = jnp.clip(keys_draw, -10.0, 10.0)
    return (query_draw, keys_draw)


def draw_queries(key, part):
    return draw_pair(key)[0].astype(jnp.bfloat16)


def draw_key_rows(key, part):
    return draw_pair(key)[1].astype(jnp.bfloat16)


def shard_levels(key, shape, pieces, least, largest):
    def one(dim, shards_of):
        draws = jax.random.uniform(jax.random.fold_in(jax.random.fold_in(key, 6), dim), (shards_of,), jnp.float32, least / len(pieces), largest / len(pieces))
        return jnp.repeat(jnp.exp(draws), shape[dim] // shards_of).reshape((-1,) + (1,) * (len(shape) - dim - 1))

    factor_of = one(*pieces[0])
    for cut in pieces[1:]:
        factor_of = factor_of * one(*cut)
    return factor_of


def normal_values(stream_key, dims, width, bound, shards=(), dtype=jnp.bfloat16):
    level = shard_levels(stream_key, dims, shards, -0.22, 0.18) if shards else 1.0
    values = jax.random.normal(stream_key, dims, jnp.float32) * width * level
    return jnp.minimum(jnp.maximum(values, -bound), bound).astype(dtype)


def setup_inputs(seed: int = 0) -> dict:
    key_list = jax.random.split(jax.random.key(seed), 7)
    queries = draw_queries(jax.random.fold_in(key_list[6], 71), 0)
    key_rows = draw_key_rows(jax.random.fold_in(key_list[6], 71), 0)
    value_rows = normal_values(key_list[2], (BATCH_SEQUENCES, SEQUENCE_TOKENS, HEADS * HEAD_DIM), 1.0, 6.0, ((1, 16), (2, 2)))
    query_tangent = normal_values(key_list[3], (BATCH_SEQUENCES, SEQUENCE_TOKENS, HEADS * HEAD_DIM), 1.0, 6.0, ((1, 16), (2, 2)))
    key_tangent = normal_values(key_list[4], (BATCH_SEQUENCES, SEQUENCE_TOKENS, HEADS * HEAD_DIM), 1.0, 6.0, ((1, 16), (2, 2)))
    out_adjoint = normal_values(key_list[5], (BATCH_SEQUENCES, SEQUENCE_TOKENS, HEADS * HEAD_DIM), 1.0, 6.0, ((1, 16), (2, 2)))
    return dict(queries=queries, key_rows=key_rows, value_rows=value_rows, query_tangent=query_tangent, key_tangent=key_tangent, out_adjoint=out_adjoint)


def head_terms(items):
    query, keyset, values_in, tquery, tkey, adjoint = items
    factor = HEAD_DIM ** -0.5
    length = query.shape[0]
    position = jnp.arange(length)
    causal = position[:, None] >= position[None, :]
    scores = factor * jnp.dot(query, keyset.T, preferred_element_type=jnp.float32)
    scores = jnp.where(causal, scores, -jnp.inf)
    top_score = jnp.max(scores, axis=1, keepdims=True)
    weights = jnp.exp(scores - top_score)
    probs = weights / jnp.sum(weights, axis=1, keepdims=True)
    tangent_scores = factor * (jnp.dot(tquery, keyset.T, preferred_element_type=jnp.float32) + jnp.dot(query, tkey.T, preferred_element_type=jnp.float32))
    mean_tangent = jnp.sum(probs * tangent_scores, axis=1, keepdims=True)
    tangent_probs = probs * (tangent_scores - mean_tangent)
    grad_probs = jnp.dot(adjoint, values_in.T, preferred_element_type=jnp.float32)
    delta = jnp.sum(probs * grad_probs, axis=1, keepdims=True)
    grad_scores = probs * (grad_probs - delta)
    tangent_delta = jnp.sum(tangent_probs * grad_probs, axis=1, keepdims=True)
    second_scores = tangent_probs * (grad_probs - delta) - probs * tangent_delta
    tprob_low = tangent_probs.astype(jnp.bfloat16)
    gscore_low = grad_scores.astype(jnp.bfloat16)
    second_low = second_scores.astype(jnp.bfloat16)
    value_hvp = jnp.dot(tprob_low.T, adjoint, preferred_element_type=jnp.float32)
    query_hvp = factor * (jnp.dot(second_low, keyset, preferred_element_type=jnp.float32) + jnp.dot(gscore_low, tkey, preferred_element_type=jnp.float32))
    key_hvp = factor * (jnp.dot(second_low.T, query, preferred_element_type=jnp.float32) + jnp.dot(gscore_low.T, tquery, preferred_element_type=jnp.float32))
    kappa = jnp.sum(tquery.astype(jnp.float32) * query_hvp) + jnp.sum(tkey.astype(jnp.float32) * key_hvp)
    return query_hvp.astype(jnp.bfloat16), key_hvp.astype(jnp.bfloat16), value_hvp.astype(jnp.bfloat16), kappa


def split_heads(tensor):
    batch_count = tensor.shape[0]
    length = tensor.shape[1]
    shaped = tensor.reshape(batch_count, length, -1, HEAD_DIM)
    return jnp.transpose(shaped, (0, 2, 1, 3)).reshape(-1, length, HEAD_DIM)


def join_heads(tensor, batch_count):
    length = tensor.shape[1]
    shaped = tensor.reshape(batch_count, -1, length, HEAD_DIM)
    return jnp.transpose(shaped, (0, 2, 1, 3)).reshape(batch_count, length, -1)


def reference(queries, key_rows, value_rows, query_tangent, key_tangent, out_adjoint):
    batch_count = queries.shape[0]
    items = tuple(split_heads(tensor) for tensor in (queries, key_rows, value_rows, query_tangent, key_tangent, out_adjoint))
    query_hvp, key_hvp, value_hvp, kappa = lax.map(head_terms, items)
    curvature = kappa.reshape(batch_count, -1)
    return join_heads(query_hvp, batch_count), join_heads(key_hvp, batch_count), join_heads(value_hvp, batch_count), curvature
```

```python
import functools
import math

import jax
import jax.numpy as jnp
from jax import lax
from jax.experimental import pallas as pl
from jax.experimental.pallas import tpu as pltpu
from jax.sharding import PartitionSpec as P

HEAD_DIM = 128
ROWS = 256
MESH = pl.DeviceIdType.MESH
F32 = jnp.float32
BF16 = jnp.bfloat16


def mm(left, right, dims):
    return lax.dot_general(left, right, (dims, ((), ())), preferred_element_type=F32)


def kernel(
    n,
    m,
    batch,
    local_heads,
    q_in,
    k_in,
    v_in,
    tq_in,
    tk_in,
    g_in,
    q_out,
    k_out,
    v_out,
    curv_out,
    qq,
    kk,
    gg,
    vv,
    probs_buf,
    tprobs_buf,
    hk_acc,
    hv_acc,
    staged,
    mine,
    board,
    in_send,
    in_recv,
    out_send,
    out_recv,
    board_send,
    board_recv,
):
    D = HEAD_DIM
    me = lax.axis_index("seq")
    dp = lax.axis_index("dp")
    tokens = q_in.shape[1]
    length = n * tokens
    rows = min(ROWS, length)
    blocks = length // rows
    per_block = rows // tokens
    factor = D ** (-0.5)

    barrier = pltpu.get_barrier_semaphore()

    def greet(step, carry):
        other = lax.rem(dp * n + me + step, n * m)
        pl.semaphore_signal(
            barrier, inc=1, device_id=(other % n, other // n), device_id_type=MESH
        )
        return carry

    lax.fori_loop(1, n * m, greet, 0)

    order = (
        (q_in, qq, D),
        (k_in, kk, 0),
        (tq_in, qq, 0),
        (tk_in, kk, D),
        (v_in, vv, 0),
        (g_in, gg, 0),
    )

    def landing(number, owner):
        _, buf, column = order[number]
        return buf.at[pl.ds(pl.multiple_of(owner * tokens, tokens), tokens), column : column + D]

    def piece(number, pair):
        source = order[number][0]
        b = pair // local_heads
        h = pair % local_heads
        return source.at[b, :, pl.ds(pl.multiple_of(h * D, D), D)]

    for number in range(6):
        pltpu.make_async_copy(piece(number, me), landing(number, me), in_recv.at[number]).start()

    pl.semaphore_wait(barrier, n * m - 1)

    def far_first(step):
        half = (step + 1) // 2
        hop = n // 2 + half * (1 - 2 * (step % 2))
        return (me + hop) % n

    for number in range(6):

        def send(step, carry, number=number):
            other = far_first(step)
            pltpu.make_async_remote_copy(
                src_ref=piece(number, other),
                dst_ref=landing(number, me),
                send_sem=in_send.at[number],
                recv_sem=in_recv.at[number],
                device_id=(other, dp),
                device_id_type=MESH,
            ).start()
            return carry

        lax.fori_loop(0, n - 1, send, 0)

    def arrived(number):
        _, buf, column = order[number]
        whole = buf.at[:, column : column + D]
        pltpu.make_async_copy(whole, whole, in_recv.at[number]).wait()

    my_batch = me // local_heads
    my_head = me % local_heads
    my_columns = pl.ds(pl.multiple_of(my_head * D, D), D)
    outs = (q_out, k_out, v_out)

    arrived(0)
    arrived(1)
    for block in range(blocks):
        start = block * rows
        width = start + rows
        part = slice(start, width)
        scores = mm(qq[part, D:], kk[:width, :D], ((1,), (1,)))
        row = lax.broadcasted_iota(jnp.int32, (rows, width), 0) + start
        col = lax.broadcasted_iota(jnp.int32, (rows, width), 1)
        scores = jnp.where(row >= col, scores, -jnp.inf)
        top = jnp.max(scores, axis=1, keepdims=True)
        weights = jnp.exp2((scores - top) * (factor * math.log2(math.e)))
        scale = 1.0 / jnp.sum(weights, axis=1, keepdims=True)
        probs_buf[part, :width] = weights * scale

    arrived(2)
    arrived(3)
    for block in range(blocks):
        start = block * rows
        width = start + rows
        part = slice(start, width)
        probs = probs_buf[part, :width]
        tangent = factor * mm(qq[part, :], kk[:width, :], ((1,), (1,)))
        mean = jnp.sum(probs * tangent, axis=1, keepdims=True)
        tprobs_buf[part, :width] = probs * (tangent - mean)

    arrived(4)
    arrived(5)
    kappa = jnp.zeros((1, 1), F32)
    for block in reversed(range(blocks)):
        start = block * rows
        width = start + rows
        part = slice(start, width)
        probs = probs_buf[part, :width]
        tprobs = tprobs_buf[part, :width]
        adj = gg[part, :]
        gprobs = mm(adj, vv[:width, :], ((1,), (1,)))
        delta = jnp.sum(probs * gprobs, axis=1, keepdims=True)
        centered = gprobs - delta
        tdelta = jnp.sum(tprobs * gprobs, axis=1, keepdims=True)
        tprob_low = tprobs.astype(BF16)
        gscore_low = (probs * centered).astype(BF16)
        second_low = (tprobs * centered - probs * tdelta).astype(BF16)
        hv = mm(tprob_low, adj, ((0,), (0,)))
        hq = factor * (
            mm(second_low, kk[:width, :D], ((1,), (0,)))
            + mm(gscore_low, kk[:width, D:], ((1,), (0,)))
        )
        hk = factor * (
            mm(second_low, qq[part, D:], ((0,), (0,)))
            + mm(gscore_low, qq[part, :D], ((0,), (0,)))
        )
        if block == blocks - 1:
            hk_acc[...] = hk
            hv_acc[...] = hv
        else:
            hk_acc[:width, :] += hk
            hv_acc[:width, :] += hv
        hk_done = hk_acc[part, :]
        kappa += jnp.sum(
            qq[part, :D].astype(F32) * hq + kk[part, D:].astype(F32) * hk_done, keepdims=True
        )
        staged[0, part, :] = hq.astype(BF16)
        staged[1, part, :] = hk_done.astype(BF16)
        staged[2, part, :] = hv_acc[part, :].astype(BF16)

        def give(step, carry, block=block):
            other = block * per_block + step
            mine_rows = pl.ds(pl.multiple_of(other * tokens, tokens), tokens)

            @pl.when(other == me)
            def _():
                for number in range(3):
                    pltpu.make_async_copy(
                        staged.at[number, mine_rows, :],
                        outs[number].at[my_batch, :, my_columns],
                        out_recv.at[number],
                    ).start()

            @pl.when(other != me)
            def _():
                for number in range(3):
                    pltpu.make_async_remote_copy(
                        src_ref=staged.at[number, mine_rows, :],
                        dst_ref=outs[number].at[my_batch, :, my_columns],
                        send_sem=out_send.at[number],
                        recv_sem=out_recv.at[number],
                        device_id=(other, dp),
                        device_id_type=MESH,
                    ).start()

            return carry

        lax.fori_loop(0, per_block, give, 0)

    shape = mine.shape
    at_row = lax.broadcasted_iota(jnp.int32, shape, 0) == my_batch
    at_col = lax.broadcasted_iota(jnp.int32, shape, 1) == dp * local_heads + my_head
    mine[...] = jnp.where(jnp.logical_and(at_row, at_col), kappa, 0.0)
    slot = dp * n + me

    def tell(step, carry):
        other = (slot + step) % (n * m)
        pltpu.make_async_remote_copy(
            src_ref=mine,
            dst_ref=board.at[slot],
            send_sem=board_send,
            recv_sem=board_recv,
            device_id=(other % n, other // n),
            device_id_type=MESH,
        ).start()
        return carry

    pltpu.make_async_copy(mine, board.at[slot], board_recv).start()
    lax.fori_loop(1, n * m, tell, 0)

    for number in range(6):
        _, buf, column = order[number]
        gone = buf.at[: (n - 1) * tokens, column : column + D]
        pltpu.make_async_copy(gone, gone, in_send.at[number]).wait()
    for number in range(3):
        gone = staged.at[number, : (n - 1) * tokens, :]
        pltpu.make_async_copy(gone, gone, out_send.at[number]).wait()
    gone = board.at[: n * m - 1]
    pltpu.make_async_copy(gone, gone, board_send).wait()
    pltpu.make_async_copy(board, board, board_recv).wait()
    total = jnp.sum(board[...], axis=0)
    curv_out[...] = total[: curv_out.shape[0], : curv_out.shape[1]]
    for number in range(3):
        pltpu.make_async_copy(outs[number], outs[number], out_recv.at[number]).wait()


def local(n, m, queries, key_rows, value_rows, query_tangent, key_tangent, out_adjoint):
    batch, tokens, width = queries.shape
    local_heads = width // HEAD_DIM
    length = n * tokens
    heads = local_heads * m
    board_shape = (-(-batch // 8) * 8, -(-heads // 128) * 128)
    result = jax.ShapeDtypeStruct(queries.shape, BF16)
    D = HEAD_DIM
    return pl.pallas_call(
        functools.partial(kernel, n, m, batch, local_heads),
        out_shape=(result, result, result, jax.ShapeDtypeStruct((batch, heads), F32)),
        in_specs=[pl.BlockSpec(memory_space=pl.ANY)] * 6,
        out_specs=(
            pl.BlockSpec(memory_space=pl.ANY),
            pl.BlockSpec(memory_space=pl.ANY),
            pl.BlockSpec(memory_space=pl.ANY),
            pl.BlockSpec(memory_space=pltpu.VMEM),
        ),
        scratch_shapes=[
            pltpu.VMEM((length, 2 * D), BF16),
            pltpu.VMEM((length, 2 * D), BF16),
            pltpu.VMEM((length, D), BF16),
            pltpu.VMEM((length, D), BF16),
            pltpu.VMEM((length, length), F32),
            pltpu.VMEM((length, length), F32),
            pltpu.VMEM((length, D), F32),
            pltpu.VMEM((length, D), F32),
            pltpu.VMEM((3, length, D), BF16),
            pltpu.VMEM(board_shape, F32),
            pltpu.VMEM((n * m,) + board_shape, F32),
            pltpu.SemaphoreType.DMA((6,)),
            pltpu.SemaphoreType.DMA((6,)),
            pltpu.SemaphoreType.DMA((3,)),
            pltpu.SemaphoreType.DMA((3,)),
            pltpu.SemaphoreType.DMA,
            pltpu.SemaphoreType.DMA,
        ],
        compiler_params=pltpu.CompilerParams(
            collective_id=0, has_side_effects=True, vmem_limit_bytes=56 * 1024 * 1024
        ),
    )(queries, key_rows, value_rows, query_tangent, key_tangent, out_adjoint)


def solution(mesh):
    split = P(None, "seq", "dp")
    return jax.shard_map(
        functools.partial(local, mesh.shape["seq"], mesh.shape["dp"]),
        mesh=mesh,
        in_specs=(split,) * 6,
        out_specs=(split, split, split, P()),
        check_vma=False,
    )
```

```python
import functools
import math

import jax
import jax.numpy as jnp
from jax import lax
from jax.experimental import pallas as pl
from jax.experimental.pallas import tpu as pltpu
from jax.sharding import PartitionSpec as P

HEAD_DIM = 128
ROWS = 256
SLOTS = 3
MESH = pl.DeviceIdType.MESH
F32 = jnp.float32
BF16 = jnp.bfloat16


def mm(left, right, dims):
    return lax.dot_general(left, right, (dims, ((), ())), preferred_element_type=F32)


def kernel(
    n,
    m,
    local_heads,
    q_in,
    k_in,
    v_in,
    tq_in,
    tk_in,
    g_in,
    q_out,
    k_out,
    v_out,
    curv_out,
    qq,
    kk,
    gg,
    vv,
    hk_acc,
    hv_acc,
    q_staged,
    k_staged,
    v_staged,
    k_low,
    v_low,
    mine,
    board,
    in_send,
    in_recv,
    out_send,
    out_recv,
    low_recv,
    board_send,
    board_recv,
):
    D = HEAD_DIM
    me = lax.axis_index("seq")
    dp = lax.axis_index("dp")
    tokens = q_in.shape[1]
    quarter = n // 4
    half = n // 2
    length = n * tokens
    upper = half * tokens
    rows = min(ROWS, upper)
    per_block = rows // tokens
    factor = D ** (-0.5)
    level = me // quarter
    ring = me % quarter
    near = ((level + 1) // 2) % 2
    low = level < 2
    slots = 1 + (SLOTS - 1) * near

    barrier = pltpu.get_barrier_semaphore()

    def greet(step, carry):
        other = lax.rem(dp * n + me + step, n * m)
        pl.semaphore_signal(
            barrier, inc=1, device_id=(other % n, other // n), device_id_type=MESH
        )
        return carry

    lax.fori_loop(1, n * m, greet, 0)

    tensors = (
        (k_in, kk, 0, length),
        (tk_in, kk, D, length),
        (v_in, vv, 0, length),
        (q_in, qq, D, upper),
        (tq_in, qq, 0, upper),
        (g_in, gg, 0, upper),
    )

    def columns(pair):
        return pl.ds(pl.multiple_of((pair % local_heads) * D, D), D)

    def feed(number, pair, slot, home, row):
        source, buf, column, span = tensors[number]
        src = source.at[pair // local_heads, :, columns(pair)]
        at = pl.multiple_of(slot * span + row, tokens)
        dst = buf.at[pl.ds(at, tokens), column : column + D]

        @pl.when(home == me)
        def _():
            pltpu.make_async_copy(src, dst, in_recv.at[slot, number]).start()

        @pl.when(home != me)
        def _():
            pltpu.make_async_remote_copy(
                src_ref=src,
                dst_ref=dst,
                send_sem=in_send.at[number],
                recv_sem=in_recv.at[slot, number],
                device_id=(home, dp),
                device_id_type=MESH,
            ).start()

    pl.semaphore_wait(barrier, n * m - 1)

    for group in (0, 3, 1, 2):
        far = 1 if group == 3 else 0
        slot = 0 if far else group

        def send(step, carry, group=group, far=far, slot=slot):
            spot = (me + step) % quarter
            pair = group * quarter + spot
            low_home = (1 - far) * quarter + spot
            high_home = half + far * quarter + spot

            @pl.when(low)
            def _():
                for number in range(3):
                    feed(number, pair, slot, high_home, me * tokens)
                for number in range(6):
                    feed(number, pair, slot, low_home, me * tokens)

            @pl.when(jnp.logical_not(low))
            def _():
                for number in range(3):
                    feed(number, pair, slot, high_home, me * tokens)
                for number in range(3, 6):
                    feed(number, pair, slot, high_home, (me - half) * tokens)

            return carry

        lax.fori_loop(0, quarter, send, 0)

    shape = mine.shape
    mine[...] = jnp.zeros(shape, F32)

    def ship(staged, at, other, dst, number, recv):
        src = staged.at[pl.ds(pl.multiple_of(at, tokens), tokens), :]

        @pl.when(other == me)
        def _():
            pltpu.make_async_copy(src, dst, recv).start()

        @pl.when(other != me)
        def _():
            pltpu.make_async_remote_copy(
                src_ref=src,
                dst_ref=dst,
                send_sem=out_send.at[number],
                recv_sem=recv,
                device_id=(other, dp),
                device_id_type=MESH,
            ).start()

    def work(slot, base):
        group = near * slot + (1 - near) * 3
        pair = group * quarter + ring
        batch = pair // local_heads
        cols = columns(pair)
        keys = base + upper
        top_rows = pl.multiple_of(slot * upper, rows)
        top_keys = pl.multiple_of(slot * length, rows)

        def arrived(number, count):
            _, buf, column, span = tensors[number]
            whole = buf.at[:count, column : column + D]
            pltpu.make_async_copy(whole, whole, in_recv.at[slot, number]).wait()

        for number in range(6):
            arrived(number, keys if number < 3 else upper)

        kappa = jnp.zeros((1, 1), F32)
        for start in reversed(range(base, keys, rows)):
            width = start + rows
            here = pl.ds(pl.multiple_of(top_rows + (start - base), rows), rows)
            seen = pl.ds(top_keys, width)
            both = qq[here, :]
            adj = gg[here, :]
            both_keys = kk[seen, :]
            scores = mm(both[:, D:], both_keys[:, :D], ((1,), (1,)))
            row = lax.broadcasted_iota(jnp.int32, (rows, width), 0) + start
            col = lax.broadcasted_iota(jnp.int32, (rows, width), 1)
            scores = jnp.where(row >= col, scores, -jnp.inf)
            top = jnp.max(scores, axis=1, keepdims=True)
            weights = jnp.exp2((scores - top) * (factor * math.log2(math.e)))
            probs = weights * (1.0 / jnp.sum(weights, axis=1, keepdims=True))
            tangent = factor * mm(both, both_keys, ((1,), (1,)))
            mean = jnp.sum(probs * tangent, axis=1, keepdims=True)
            tprobs = probs * (tangent - mean)
            gprobs = mm(adj, vv[seen, :], ((1,), (1,)))
            delta = jnp.sum(probs * gprobs, axis=1, keepdims=True)
            centered = gprobs - delta
            tdelta = jnp.sum(tprobs * gprobs, axis=1, keepdims=True)
            tprob_low = tprobs.astype(BF16)
            gscore_low = (probs * centered).astype(BF16)
            second_low = (tprobs * centered - probs * tdelta).astype(BF16)
            hv = mm(tprob_low, adj, ((0,), (0,)))
            hq = factor * (
                mm(second_low, both_keys[:, :D], ((1,), (0,)))
                + mm(gscore_low, both_keys[:, D:], ((1,), (0,)))
            )
            hk = factor * (
                mm(second_low, both[:, D:], ((0,), (0,)))
                + mm(gscore_low, both[:, :D], ((0,), (0,)))
            )
            if width == keys:
                hk_acc[:keys, :] = hk
                hv_acc[:keys, :] = hv
            else:
                hk_acc[:width, :] += hk
                hv_acc[:width, :] += hv
            kappa += jnp.sum(both[:, :D].astype(F32) * hq, keepdims=True)
            q_staged[here, :] = hq.astype(BF16)

            done = start if start > base else 0
            count = width - done
            span = slice(done, width)
            area = pl.ds(pl.multiple_of(top_keys + done, rows), count)
            hk_done = hk_acc[span, :]
            kappa += jnp.sum(kk[area, D:].astype(F32) * hk_done, keepdims=True)
            k_staged[area, :] = hk_done.astype(BF16)
            v_staged[area, :] = hv_acc[span, :].astype(BF16)

            def give_q(step, carry, start=start):
                other = start // tokens + step
                at = top_rows + other * tokens - base
                ship(q_staged, at, other, q_out.at[batch, :, cols], 0, out_recv.at[0])
                return carry

            def give_kv(step, carry, done=done):
                other = done // tokens + step
                at = top_keys + other * tokens
                if base:
                    ship(k_staged, at, other, k_out.at[batch, :, cols], 1, out_recv.at[1])
                    ship(v_staged, at, other, v_out.at[batch, :, cols], 2, out_recv.at[2])
                else:
                    ship(k_staged, at, other, k_low.at[batch, :, cols], 1, low_recv.at[0])
                    ship(v_staged, at, other, v_low.at[batch, :, cols], 2, low_recv.at[1])
                return carry

            lax.fori_loop(0, count // tokens, give_kv, 0)
            lax.fori_loop(0, per_block, give_q, 0)

        at_row = lax.broadcasted_iota(jnp.int32, shape, 0) == batch
        at_col = (
            lax.broadcasted_iota(jnp.int32, shape, 1) == dp * local_heads + pair % local_heads
        )
        mine[...] += jnp.where(jnp.logical_and(at_row, at_col), kappa, 0.0)

    def all_slots(base):
        def one(slot, carry):
            work(slot, base)
            return carry

        lax.fori_loop(0, slots, one, 0)

    @pl.when(low)
    def _():
        all_slots(0)

    @pl.when(jnp.logical_not(low))
    def _():
        all_slots(upper)

    place = dp * n + me

    def tell(step, carry):
        other = (place + step) % (n * m)
        pltpu.make_async_remote_copy(
            src_ref=mine,
            dst_ref=board.at[place],
            send_sem=board_send,
            recv_sem=board_recv,
            device_id=(other % n, other // n),
            device_id_type=MESH,
        ).start()
        return carry

    pltpu.make_async_copy(mine, board.at[place], board_recv).start()
    lax.fori_loop(1, n * m, tell, 0)

    def gone(units, sem):
        sent = vv.at[: units * tokens, :]
        pltpu.make_async_copy(sent, sent, sem).wait()

    for is_low in (True, False):
        for count, is_near in ((SLOTS, 1), (1, 0)):

            @pl.when(jnp.logical_and(low == is_low, near == is_near))
            def _(is_low=is_low, count=count):
                for number in range(6):
                    gone(n - count + (n if is_low and number < 3 else 0), in_send.at[number])
                gone(count * (half - 1), out_send.at[0])
                for number in (1, 2):
                    gone(count * ((half if is_low else n) - 1), out_send.at[number])

    sent = board.at[: n * m - 1]
    pltpu.make_async_copy(sent, sent, board_send).wait()

    pltpu.make_async_copy(q_out, q_out, out_recv.at[0]).wait()
    pltpu.make_async_copy(k_out, k_out, out_recv.at[1]).wait()
    pltpu.make_async_copy(v_out, v_out, out_recv.at[2]).wait()

    @pl.when(low)
    def _():
        pltpu.make_async_copy(k_low, k_low, low_recv.at[0]).wait()
        pltpu.make_async_copy(v_low, v_low, low_recv.at[1]).wait()
        k_out[...] = (k_out[...].astype(F32) + k_low[...].astype(F32)).astype(BF16)
        v_out[...] = (v_out[...].astype(F32) + v_low[...].astype(F32)).astype(BF16)

    pltpu.make_async_copy(board, board, board_recv).wait()
    total = jnp.sum(board[...], axis=0)
    curv_out[...] = total[: curv_out.shape[0], : curv_out.shape[1]]


def local(n, m, queries, key_rows, value_rows, query_tangent, key_tangent, out_adjoint):
    batch, tokens, width = queries.shape
    local_heads = width // HEAD_DIM
    length = n * tokens
    heads = local_heads * m
    board_shape = (-(-batch // 8) * 8, -(-heads // 128) * 128)
    result = jax.ShapeDtypeStruct(queries.shape, BF16)
    D = HEAD_DIM
    return pl.pallas_call(
        functools.partial(kernel, n, m, local_heads),
        out_shape=(result, result, result, jax.ShapeDtypeStruct((batch, heads), F32)),
        in_specs=[pl.BlockSpec(memory_space=pl.ANY)] * 6,
        out_specs=(pl.BlockSpec(memory_space=pltpu.VMEM),) * 4,
        scratch_shapes=[
            pltpu.VMEM((SLOTS * length // 2, 2 * D), BF16),
            pltpu.VMEM((SLOTS * length, 2 * D), BF16),
            pltpu.VMEM((SLOTS * length // 2, D), BF16),
            pltpu.VMEM((SLOTS * length, D), BF16),
            pltpu.VMEM((length, D), F32),
            pltpu.VMEM((length, D), F32),
            pltpu.VMEM((SLOTS * length // 2, D), BF16),
            pltpu.VMEM((SLOTS * length, D), BF16),
            pltpu.VMEM((SLOTS * length, D), BF16),
            pltpu.VMEM(queries.shape, BF16),
            pltpu.VMEM(queries.shape, BF16),
            pltpu.VMEM(board_shape, F32),
            pltpu.VMEM((n * m,) + board_shape, F32),
            pltpu.SemaphoreType.DMA((6,)),
            pltpu.SemaphoreType.DMA((SLOTS, 6)),
            pltpu.SemaphoreType.DMA((3,)),
            pltpu.SemaphoreType.DMA((3,)),
            pltpu.SemaphoreType.DMA((2,)),
            pltpu.SemaphoreType.DMA,
            pltpu.SemaphoreType.DMA,
        ],
        compiler_params=pltpu.CompilerParams(
            collective_id=0, has_side_effects=True, vmem_limit_bytes=56 * 1024 * 1024
        ),
    )(queries, key_rows, value_rows, query_tangent, key_tangent, out_adjoint)


def solution(mesh):
    split = P(None, "seq", "dp")
    return jax.shard_map(
        functools.partial(local, mesh.shape["seq"], mesh.shape["dp"]),
        mesh=mesh,
        in_specs=(split,) * 6,
        out_specs=(split, split, split, P()),
        check_vma=False,
    )
```

```python
import functools
import math

import jax
import jax.numpy as jnp
from jax import lax
from jax.experimental import pallas as pl
from jax.experimental.pallas import tpu as pltpu
from jax.sharding import PartitionSpec as P

HEAD_DIM = 128
ROWS = 256
SLOTS = 3
MESH = pl.DeviceIdType.MESH
F32 = jnp.float32
BF16 = jnp.bfloat16


def mm(left, right, dims):
    return lax.dot_general(left, right, (dims, ((), ())), preferred_element_type=F32)


def kernel(
    n,
    m,
    local_heads,
    q_in,
    k_in,
    v_in,
    tq_in,
    tk_in,
    g_in,
    q_out,
    k_out,
    v_out,
    curv_out,
    qq,
    kk,
    gg,
    vv,
    relay,
    hk_acc,
    hv_acc,
    q_staged,
    k_staged,
    v_staged,
    k_low,
    v_low,
    mine,
    board,
    in_send,
    in_recv,
    relay_recv,
    out_send,
    out_recv,
    low_recv,
    board_send,
    board_recv,
):
    D = HEAD_DIM
    me = lax.axis_index("seq")
    dp = lax.axis_index("dp")
    tokens = q_in.shape[1]
    quarter = n // 4
    half = n // 2
    length = n * tokens
    upper = half * tokens
    rows = min(ROWS, upper)
    per_block = rows // tokens
    factor = D ** (-0.5)
    level = me // quarter
    ring = me % quarter
    near = ((level + 1) // 2) % 2
    low = level < 2
    slots = 1 + (SLOTS - 1) * near

    barrier = pltpu.get_barrier_semaphore()

    def greet(step, carry):
        other = lax.rem(dp * n + me + step, n * m)
        pl.semaphore_signal(
            barrier, inc=1, device_id=(other % n, other // n), device_id_type=MESH
        )
        return carry

    lax.fori_loop(1, n * m, greet, 0)

    tensors = (
        (k_in, kk, 0, length),
        (tk_in, kk, D, length),
        (v_in, vv, 0, length),
        (q_in, qq, D, upper),
        (tq_in, qq, 0, upper),
        (g_in, gg, 0, upper),
    )

    def columns(pair):
        return pl.ds(pl.multiple_of((pair % local_heads) * D, D), D)

    def cut(number, pair):
        return tensors[number][0].at[pair // local_heads, :, columns(pair)]

    def feed(number, src, slot, home, row):
        _, buf, column, span = tensors[number]
        at = pl.multiple_of(slot * span + row, tokens)
        dst = buf.at[pl.ds(at, tokens), column : column + D]

        @pl.when(home == me)
        def _():
            pltpu.make_async_copy(src, dst, in_recv.at[slot, number]).start()

        @pl.when(home != me)
        def _():
            pltpu.make_async_remote_copy(
                src_ref=src,
                dst_ref=dst,
                send_sem=in_send.at[number],
                recv_sem=in_recv.at[slot, number],
                device_id=(home, dp),
                device_id_type=MESH,
            ).start()

    pl.semaphore_wait(barrier, n * m - 1)

    side = (me // 2) % 2
    partner = (me // 4) * 4 + (me + 2) % 4

    def spot_of(step, column):
        return (step // 2) * 4 + 2 * column + step % 2

    def swap(step, carry):
        group = step // (quarter // 2)
        pair = group * quarter + spot_of(step % (quarter // 2), 1 - side)
        for number in range(6):
            at = pl.multiple_of((step * 6 + number) * tokens, tokens)
            pltpu.make_async_remote_copy(
                src_ref=cut(number, pair),
                dst_ref=relay.at[pl.ds(at, tokens), :],
                send_sem=in_send.at[number],
                recv_sem=relay_recv.at[group],
                device_id=(partner, dp),
                device_id_type=MESH,
            ).start()
        return carry

    def forward(group, relayed):
        far = 1 if group == 3 else 0
        slot = 0 if far else group
        owner = partner if relayed else me
        first = group * (quarter // 2)
        if relayed:
            batch_of = 6 * (quarter // 2) * tokens
            all_of = relay.at[group * batch_of : (group + 1) * batch_of, :]
            pltpu.make_async_copy(all_of, all_of, relay_recv.at[group]).wait()

        def send(step, carry):
            spot = spot_of(step, side)
            pair = group * quarter + spot
            low_home = (1 - far) * quarter + spot
            high_home = half + far * quarter + spot

            def source(number):
                if relayed:
                    at = pl.multiple_of(((first + step) * 6 + number) * tokens, tokens)
                    return relay.at[pl.ds(at, tokens), :]
                return cut(number, pair)

            @pl.when(low)
            def _():
                for number in range(3):
                    feed(number, source(number), slot, high_home, owner * tokens)
                for number in range(6):
                    feed(number, source(number), slot, low_home, owner * tokens)

            @pl.when(jnp.logical_not(low))
            def _():
                for number in range(3):
                    feed(number, source(number), slot, high_home, owner * tokens)
                for number in range(3, 6):
                    feed(number, source(number), slot, high_home, (owner - half) * tokens)

            return carry

        lax.fori_loop(0, quarter // 2, send, 0)

    lax.fori_loop(0, half, swap, 0)
    forward(0, False)
    forward(3, False)
    forward(0, True)
    forward(3, True)
    forward(1, False)
    forward(1, True)
    forward(2, False)
    forward(2, True)

    shape = mine.shape
    mine[...] = jnp.zeros(shape, F32)

    def ship(staged, at, other, dst, number, recv):
        src = staged.at[pl.ds(pl.multiple_of(at, tokens), tokens), :]

        @pl.when(other == me)
        def _():
            pltpu.make_async_copy(src, dst, recv).start()

        @pl.when(other != me)
        def _():
            pltpu.make_async_remote_copy(
                src_ref=src,
                dst_ref=dst,
                send_sem=out_send.at[number],
                recv_sem=recv,
                device_id=(other, dp),
                device_id_type=MESH,
            ).start()

    def work(slot, base):
        group = near * slot + (1 - near) * 3
        pair = group * quarter + ring
        batch = pair // local_heads
        cols = columns(pair)
        keys = base + upper
        top_rows = pl.multiple_of(slot * upper, rows)
        top_keys = pl.multiple_of(slot * length, rows)

        def arrived(number, count):
            _, buf, column, span = tensors[number]
            whole = buf.at[:count, column : column + D]
            pltpu.make_async_copy(whole, whole, in_recv.at[slot, number]).wait()

        for number in range(6):
            arrived(number, keys if number < 3 else upper)

        kappa = jnp.zeros((1, 1), F32)
        for start in reversed(range(base, keys, rows)):
            width = start + rows
            here = pl.ds(pl.multiple_of(top_rows + (start - base), rows), rows)
            seen = pl.ds(top_keys, width)
            both = qq[here, :]
            adj = gg[here, :]
            both_keys = kk[seen, :]
            scores = mm(both[:, D:], both_keys[:, :D], ((1,), (1,)))
            row = lax.broadcasted_iota(jnp.int32, (rows, width), 0) + start
            col = lax.broadcasted_iota(jnp.int32, (rows, width), 1)
            scores = jnp.where(row >= col, scores, -jnp.inf)
            top = jnp.max(scores, axis=1, keepdims=True)
            weights = jnp.exp2((scores - top) * (factor * math.log2(math.e)))
            probs = weights * (1.0 / jnp.sum(weights, axis=1, keepdims=True))
            tangent = factor * mm(both, both_keys, ((1,), (1,)))
            mean = jnp.sum(probs * tangent, axis=1, keepdims=True)
            tprobs = probs * (tangent - mean)
            gprobs = mm(adj, vv[seen, :], ((1,), (1,)))
            delta = jnp.sum(probs * gprobs, axis=1, keepdims=True)
            centered = gprobs - delta
            tdelta = jnp.sum(tprobs * gprobs, axis=1, keepdims=True)
            tprob_low = tprobs.astype(BF16)
            gscore_low = (probs * centered).astype(BF16)
            second_low = (tprobs * centered - probs * tdelta).astype(BF16)
            hv = mm(tprob_low, adj, ((0,), (0,)))
            hq = factor * (
                mm(second_low, both_keys[:, :D], ((1,), (0,)))
                + mm(gscore_low, both_keys[:, D:], ((1,), (0,)))
            )
            hk = factor * (
                mm(second_low, both[:, D:], ((0,), (0,)))
                + mm(gscore_low, both[:, :D], ((0,), (0,)))
            )
            if width == keys:
                hk_acc[:keys, :] = hk
                hv_acc[:keys, :] = hv
            else:
                hk_acc[:width, :] += hk
                hv_acc[:width, :] += hv
            kappa += jnp.sum(both[:, :D].astype(F32) * hq, keepdims=True)
            q_staged[here, :] = hq.astype(BF16)

            done = start if start > base else 0
            count = width - done
            span = slice(done, width)
            area = pl.ds(pl.multiple_of(top_keys + done, rows), count)
            hk_done = hk_acc[span, :]
            kappa += jnp.sum(kk[area, D:].astype(F32) * hk_done, keepdims=True)
            k_staged[area, :] = hk_done.astype(BF16)
            v_staged[area, :] = hv_acc[span, :].astype(BF16)

            def give_q(step, carry, start=start):
                other = start // tokens + step
                at = top_rows + other * tokens - base
                ship(q_staged, at, other, q_out.at[batch, :, cols], 0, out_recv.at[0])
                return carry

            def give_kv(step, carry, done=done):
                other = done // tokens + step
                at = top_keys + other * tokens
                if base:
                    ship(k_staged, at, other, k_out.at[batch, :, cols], 1, out_recv.at[1])
                    ship(v_staged, at, other, v_out.at[batch, :, cols], 2, out_recv.at[2])
                else:
                    ship(k_staged, at, other, k_low.at[batch, :, cols], 1, low_recv.at[0])
                    ship(v_staged, at, other, v_low.at[batch, :, cols], 2, low_recv.at[1])
                return carry

            lax.fori_loop(0, count // tokens, give_kv, 0)
            lax.fori_loop(0, per_block, give_q, 0)

        at_row = lax.broadcasted_iota(jnp.int32, shape, 0) == batch
        at_col = (
            lax.broadcasted_iota(jnp.int32, shape, 1) == dp * local_heads + pair % local_heads
        )
        mine[...] += jnp.where(jnp.logical_and(at_row, at_col), kappa, 0.0)

    def all_slots(base):
        def one(slot, carry):
            work(slot, base)
            return carry

        lax.fori_loop(0, slots, one, 0)

    @pl.when(low)
    def _():
        all_slots(0)

    @pl.when(jnp.logical_not(low))
    def _():
        all_slots(upper)

    place = dp * n + me

    def tell(step, carry):
        other = (place + step) % (n * m)
        pltpu.make_async_remote_copy(
            src_ref=mine,
            dst_ref=board.at[place],
            send_sem=board_send,
            recv_sem=board_recv,
            device_id=(other % n, other // n),
            device_id_type=MESH,
        ).start()
        return carry

    pltpu.make_async_copy(mine, board.at[place], board_recv).start()
    lax.fori_loop(1, n * m, tell, 0)

    def gone(units, sem):
        sent = vv.at[: units * tokens, :]
        pltpu.make_async_copy(sent, sent, sem).wait()

    for is_low in (True, False):
        for count, is_near in ((SLOTS, 1), (1, 0)):

            @pl.when(jnp.logical_and(low == is_low, near == is_near))
            def _(is_low=is_low, count=count):
                for number in range(6):
                    gone(n - 2 * count + half + (n if is_low and number < 3 else 0), in_send.at[number])
                gone(count * (half - 1), out_send.at[0])
                for number in (1, 2):
                    gone(count * ((half if is_low else n) - 1), out_send.at[number])

    sent = board.at[: n * m - 1]
    pltpu.make_async_copy(sent, sent, board_send).wait()

    pltpu.make_async_copy(q_out, q_out, out_recv.at[0]).wait()
    pltpu.make_async_copy(k_out, k_out, out_recv.at[1]).wait()
    pltpu.make_async_copy(v_out, v_out, out_recv.at[2]).wait()

    @pl.when(low)
    def _():
        pltpu.make_async_copy(k_low, k_low, low_recv.at[0]).wait()
        pltpu.make_async_copy(v_low, v_low, low_recv.at[1]).wait()
        k_out[...] = (k_out[...].astype(F32) + k_low[...].astype(F32)).astype(BF16)
        v_out[...] = (v_out[...].astype(F32) + v_low[...].astype(F32)).astype(BF16)

    pltpu.make_async_copy(board, board, board_recv).wait()
    total = jnp.sum(board[...], axis=0)
    curv_out[...] = total[: curv_out.shape[0], : curv_out.shape[1]]


def hand_over(q, k, v, curv, q_out, k_out, v_out, curv_out, held, read, written):
    batch = q.shape[0]
    parts = [(number, b) for number in range(3) for b in range(batch)]
    sources, outs = (q, k, v), (q_out, k_out, v_out)
    reads, writes = [], []
    for number, b in parts:
        reads.append(
            pltpu.make_async_copy(sources[number].at[b], held.at[number, b], read.at[number, b])
        )
        writes.append(
            pltpu.make_async_copy(held.at[number, b], outs[number].at[b], written.at[number, b])
        )
    for copy in reads:
        copy.start()
    curv_out[...] = curv[...]
    for first, second in zip(reads, writes):
        first.wait()
        second.start()
    for copy in writes:
        copy.wait()


def local(n, m, queries, key_rows, value_rows, query_tangent, key_tangent, out_adjoint):
    batch, tokens, width = queries.shape
    local_heads = width // HEAD_DIM
    length = n * tokens
    heads = local_heads * m
    board_shape = (-(-batch // 8) * 8, -(-heads // 128) * 128)
    result = jax.ShapeDtypeStruct(queries.shape, BF16)
    D = HEAD_DIM
    landed = pl.pallas_call(
        functools.partial(kernel, n, m, local_heads),
        out_shape=(result, result, result, jax.ShapeDtypeStruct((batch, heads), F32)),
        in_specs=[pl.BlockSpec(memory_space=pl.ANY)] * 6,
        out_specs=(pl.BlockSpec(memory_space=pltpu.VMEM),) * 4,
        scratch_shapes=[
            pltpu.VMEM((SLOTS * length // 2, 2 * D), BF16),
            pltpu.VMEM((SLOTS * length, 2 * D), BF16),
            pltpu.VMEM((SLOTS * length // 2, D), BF16),
            pltpu.VMEM((SLOTS * length, D), BF16),
            pltpu.VMEM((3 * length, D), BF16),
            pltpu.VMEM((length, D), F32),
            pltpu.VMEM((length, D), F32),
            pltpu.VMEM((SLOTS * length // 2, D), BF16),
            pltpu.VMEM((SLOTS * length, D), BF16),
            pltpu.VMEM((SLOTS * length, D), BF16),
            pltpu.VMEM(queries.shape, BF16),
            pltpu.VMEM(queries.shape, BF16),
            pltpu.VMEM(board_shape, F32),
            pltpu.VMEM((n * m,) + board_shape, F32),
            pltpu.SemaphoreType.DMA((6,)),
            pltpu.SemaphoreType.DMA((SLOTS, 6)),
            pltpu.SemaphoreType.DMA((4,)),
            pltpu.SemaphoreType.DMA((3,)),
            pltpu.SemaphoreType.DMA((3,)),
            pltpu.SemaphoreType.DMA((2,)),
            pltpu.SemaphoreType.DMA,
            pltpu.SemaphoreType.DMA,
        ],
        compiler_params=pltpu.CompilerParams(
            collective_id=0, has_side_effects=True, vmem_limit_bytes=56 * 1024 * 1024
        ),
    )(queries, key_rows, value_rows, query_tangent, key_tangent, out_adjoint)
    return pl.pallas_call(
        hand_over,
        out_shape=(result, result, result, jax.ShapeDtypeStruct((batch, heads), F32)),
        in_specs=[pl.BlockSpec(memory_space=pl.ANY)] * 3 + [pl.BlockSpec(memory_space=pltpu.VMEM)],
        out_specs=(
            pl.BlockSpec(memory_space=pl.ANY),
            pl.BlockSpec(memory_space=pl.ANY),
            pl.BlockSpec(memory_space=pl.ANY),
            pl.BlockSpec(memory_space=pltpu.VMEM),
        ),
        scratch_shapes=[
            pltpu.VMEM((3,) + queries.shape, BF16),
            pltpu.SemaphoreType.DMA((3, batch)),
            pltpu.SemaphoreType.DMA((3, batch)),
        ],
    )(*landed)


def solution(mesh):
    split = P(None, "seq", "dp")
    return jax.shard_map(
        functools.partial(local, mesh.shape["seq"], mesh.shape["dp"]),
        mesh=mesh,
        in_specs=(split,) * 6,
        out_specs=(split, split, split, P()),
        check_vma=False,
    )
```

```python
import functools
import math

import jax
import jax.numpy as jnp
from jax import lax
from jax.experimental import pallas as pl
from jax.experimental.pallas import tpu as pltpu
from jax.sharding import PartitionSpec as P

HEAD_DIM = 128
ROWS = 256
SLOTS = 3
MESH = pl.DeviceIdType.MESH
F32 = jnp.float32
BF16 = jnp.bfloat16


def mm(left, right, dims):
    return lax.dot_general(left, right, (dims, ((), ())), preferred_element_type=F32)


def kernel(
    n,
    m,
    local_heads,
    q_in,
    k_in,
    v_in,
    tq_in,
    tk_in,
    g_in,
    q_out,
    k_out,
    v_out,
    curv_out,
    qq,
    kk,
    gg,
    vv,
    relay,
    hk_acc,
    hv_acc,
    q_staged,
    k_staged,
    v_staged,
    k_low,
    v_low,
    mine,
    board,
    in_send,
    in_recv,
    relay_recv,
    out_send,
    out_recv,
    low_recv,
    board_send,
    board_recv,
):
    D = HEAD_DIM
    me = lax.axis_index("seq")
    dp = lax.axis_index("dp")
    tokens = q_in.shape[1]
    quarter = n // 4
    half = n // 2
    length = n * tokens
    upper = half * tokens
    rows = min(ROWS, upper)
    per_block = rows // tokens
    factor = D ** (-0.5)
    level = me // quarter
    ring = me % quarter
    near = 1 - level % 2
    low = level < 2
    slots = 1 + (SLOTS - 1) * near

    barrier = pltpu.get_barrier_semaphore()

    def greet(step, carry):
        other = lax.rem(dp * n + me + step, n * m)
        pl.semaphore_signal(
            barrier, inc=1, device_id=(other % n, other // n), device_id_type=MESH
        )
        return carry

    lax.fori_loop(1, n * m, greet, 0)

    tensors = (
        (k_in, kk, 0, length),
        (tk_in, kk, D, length),
        (v_in, vv, 0, length),
        (q_in, qq, D, upper),
        (tq_in, qq, 0, upper),
        (g_in, gg, 0, upper),
    )

    def columns(pair):
        return pl.ds(pl.multiple_of((pair % local_heads) * D, D), D)

    def cut(number, pair):
        return tensors[number][0].at[pair // local_heads, :, columns(pair)]

    def feed(number, src, slot, home, row):
        _, buf, column, span = tensors[number]
        at = pl.multiple_of(slot * span + row, tokens)
        dst = buf.at[pl.ds(at, tokens), column : column + D]

        @pl.when(home == me)
        def _():
            pltpu.make_async_copy(src, dst, in_recv.at[slot, number]).start()

        @pl.when(home != me)
        def _():
            pltpu.make_async_remote_copy(
                src_ref=src,
                dst_ref=dst,
                send_sem=in_send.at[number],
                recv_sem=in_recv.at[slot, number],
                device_id=(home, dp),
                device_id_type=MESH,
            ).start()

    pl.semaphore_wait(barrier, n * m - 1)

    side = (me // 2) % 2
    partner = (me // 4) * 4 + (me + 2) % 4

    def spot_of(step, column):
        return (step // 2) * 4 + 2 * column + step % 2

    def swap(step, carry):
        group = step // (quarter // 2)
        pair = group * quarter + spot_of(step % (quarter // 2), 1 - side)
        for number in range(6):
            at = pl.multiple_of((step * 6 + number) * tokens, tokens)
            pltpu.make_async_remote_copy(
                src_ref=cut(number, pair),
                dst_ref=relay.at[pl.ds(at, tokens), :],
                send_sem=in_send.at[number],
                recv_sem=relay_recv.at[group],
                device_id=(partner, dp),
                device_id_type=MESH,
            ).start()
        return carry

    def forward(group, relayed):
        far = 1 if group == 3 else 0
        slot = 0 if far else group
        owner = partner if relayed else me
        first = group * (quarter // 2)
        if relayed:
            batch_of = 6 * (quarter // 2) * tokens
            all_of = relay.at[group * batch_of : (group + 1) * batch_of, :]
            pltpu.make_async_copy(all_of, all_of, relay_recv.at[group]).wait()

        def send(step, carry):
            spot = spot_of(step, side)
            pair = group * quarter + spot
            low_home = far * quarter + spot
            high_home = half + far * quarter + spot

            def source(number):
                if relayed:
                    at = pl.multiple_of(((first + step) * 6 + number) * tokens, tokens)
                    return relay.at[pl.ds(at, tokens), :]
                return cut(number, pair)

            @pl.when(low)
            def _():
                for number in range(3):
                    feed(number, source(number), slot, high_home, owner * tokens)
                for number in range(6):
                    feed(number, source(number), slot, low_home, owner * tokens)

            @pl.when(jnp.logical_not(low))
            def _():
                for number in range(3):
                    feed(number, source(number), slot, high_home, owner * tokens)
                for number in range(3, 6):
                    feed(number, source(number), slot, high_home, (owner - half) * tokens)

            return carry

        lax.fori_loop(0, quarter // 2, send, 0)

    lax.fori_loop(0, half, swap, 0)
    forward(0, False)
    forward(3, False)
    forward(0, True)
    forward(3, True)
    forward(1, False)
    forward(1, True)
    forward(2, False)
    forward(2, True)

    shape = mine.shape
    mine[...] = jnp.zeros(shape, F32)

    def ship(staged, at, other, dst, number, recv):
        src = staged.at[pl.ds(pl.multiple_of(at, tokens), tokens), :]

        @pl.when(other == me)
        def _():
            pltpu.make_async_copy(src, dst, recv).start()

        @pl.when(other != me)
        def _():
            pltpu.make_async_remote_copy(
                src_ref=src,
                dst_ref=dst,
                send_sem=out_send.at[number],
                recv_sem=recv,
                device_id=(other, dp),
                device_id_type=MESH,
            ).start()

    def work(slot, base):
        group = near * slot + (1 - near) * 3
        pair = group * quarter + ring
        batch = pair // local_heads
        cols = columns(pair)
        keys = base + upper
        top_rows = pl.multiple_of(slot * upper, rows)
        top_keys = pl.multiple_of(slot * length, rows)

        def arrived(number, count):
            _, buf, column, span = tensors[number]
            whole = buf.at[:count, column : column + D]
            pltpu.make_async_copy(whole, whole, in_recv.at[slot, number]).wait()

        for number in range(6):
            arrived(number, keys if number < 3 else upper)

        kappa = jnp.zeros((1, 1), F32)
        for start in reversed(range(base, keys, rows)):
            width = start + rows
            here = pl.ds(pl.multiple_of(top_rows + (start - base), rows), rows)
            seen = pl.ds(top_keys, width)
            both = qq[here, :]
            adj = gg[here, :]
            both_keys = kk[seen, :]
            scores = mm(both[:, D:], both_keys[:, :D], ((1,), (1,)))
            row = lax.broadcasted_iota(jnp.int32, (rows, width), 0) + start
            col = lax.broadcasted_iota(jnp.int32, (rows, width), 1)
            scores = jnp.where(row >= col, scores, -jnp.inf)
            top = jnp.max(scores, axis=1, keepdims=True)
            weights = jnp.exp2((scores - top) * (factor * math.log2(math.e)))
            probs = weights * (1.0 / jnp.sum(weights, axis=1, keepdims=True))
            tangent = factor * mm(both, both_keys, ((1,), (1,)))
            mean = jnp.sum(probs * tangent, axis=1, keepdims=True)
            tprobs = probs * (tangent - mean)
            gprobs = mm(adj, vv[seen, :], ((1,), (1,)))
            delta = jnp.sum(probs * gprobs, axis=1, keepdims=True)
            centered = gprobs - delta
            tdelta = jnp.sum(tprobs * gprobs, axis=1, keepdims=True)
            tprob_low = tprobs.astype(BF16)
            gscore_low = (probs * centered).astype(BF16)
            second_low = (tprobs * centered - probs * tdelta).astype(BF16)
            hv = mm(tprob_low, adj, ((0,), (0,)))
            hq = factor * (
                mm(second_low, both_keys[:, :D], ((1,), (0,)))
                + mm(gscore_low, both_keys[:, D:], ((1,), (0,)))
            )
            hk = factor * (
                mm(second_low, both[:, D:], ((0,), (0,)))
                + mm(gscore_low, both[:, :D], ((0,), (0,)))
            )
            if width == keys:
                hk_acc[:keys, :] = hk
                hv_acc[:keys, :] = hv
            else:
                hk_acc[:width, :] += hk
                hv_acc[:width, :] += hv
            kappa += jnp.sum(both[:, :D].astype(F32) * hq, keepdims=True)
            q_staged[here, :] = hq.astype(BF16)

            done = start if start > base else 0
            count = width - done
            span = slice(done, width)
            area = pl.ds(pl.multiple_of(top_keys + done, rows), count)
            hk_done = hk_acc[span, :]
            kappa += jnp.sum(kk[area, D:].astype(F32) * hk_done, keepdims=True)
            k_staged[area, :] = hk_done.astype(BF16)
            v_staged[area, :] = hv_acc[span, :].astype(BF16)

            def give_q(step, carry, start=start):
                other = start // tokens + step
                at = top_rows + other * tokens - base
                ship(q_staged, at, other, q_out.at[batch, :, cols], 0, out_recv.at[0])
                return carry

            def give_kv(step, carry, done=done):
                other = done // tokens + step
                at = top_keys + other * tokens
                if base:
                    ship(k_staged, at, other, k_out.at[batch, :, cols], 1, out_recv.at[1])
                    ship(v_staged, at, other, v_out.at[batch, :, cols], 2, out_recv.at[2])
                else:
                    ship(k_staged, at, other, k_low.at[batch, :, cols], 1, low_recv.at[0])
                    ship(v_staged, at, other, v_low.at[batch, :, cols], 2, low_recv.at[1])
                return carry

            lax.fori_loop(0, count // tokens, give_kv, 0)
            lax.fori_loop(0, per_block, give_q, 0)

        at_row = lax.broadcasted_iota(jnp.int32, shape, 0) == batch
        at_col = (
            lax.broadcasted_iota(jnp.int32, shape, 1) == dp * local_heads + pair % local_heads
        )
        mine[...] += jnp.where(jnp.logical_and(at_row, at_col), kappa, 0.0)

    def all_slots(base):
        def one(slot, carry):
            work(slot, base)
            return carry

        lax.fori_loop(0, slots, one, 0)

    @pl.when(low)
    def _():
        all_slots(0)

    @pl.when(jnp.logical_not(low))
    def _():
        all_slots(upper)

    place = dp * n + me

    def tell(step, carry):
        other = (place + step) % (n * m)
        pltpu.make_async_remote_copy(
            src_ref=mine,
            dst_ref=board.at[place],
            send_sem=board_send,
            recv_sem=board_recv,
            device_id=(other % n, other // n),
            device_id_type=MESH,
        ).start()
        return carry

    pltpu.make_async_copy(mine, board.at[place], board_recv).start()
    lax.fori_loop(1, n * m, tell, 0)

    def gone(units, sem):
        sent = vv.at[: units * tokens, :]
        pltpu.make_async_copy(sent, sent, sem).wait()

    for is_low in (True, False):
        for count, is_near in ((SLOTS, 1), (1, 0)):

            @pl.when(jnp.logical_and(low == is_low, near == is_near))
            def _(is_low=is_low, count=count):
                for number in range(6):
                    gone(n - 2 * count + half + (n if is_low and number < 3 else 0), in_send.at[number])
                gone(count * (half - 1), out_send.at[0])
                for number in (1, 2):
                    gone(count * ((half if is_low else n) - 1), out_send.at[number])

    sent = board.at[: n * m - 1]
    pltpu.make_async_copy(sent, sent, board_send).wait()

    pltpu.make_async_copy(q_out, q_out, out_recv.at[0]).wait()
    pltpu.make_async_copy(k_out, k_out, out_recv.at[1]).wait()
    pltpu.make_async_copy(v_out, v_out, out_recv.at[2]).wait()

    @pl.when(low)
    def _():
        pltpu.make_async_copy(k_low, k_low, low_recv.at[0]).wait()
        pltpu.make_async_copy(v_low, v_low, low_recv.at[1]).wait()
        k_out[...] = (k_out[...].astype(F32) + k_low[...].astype(F32)).astype(BF16)
        v_out[...] = (v_out[...].astype(F32) + v_low[...].astype(F32)).astype(BF16)

    pltpu.make_async_copy(board, board, board_recv).wait()
    total = jnp.sum(board[...], axis=0)
    curv_out[...] = total[: curv_out.shape[0], : curv_out.shape[1]]


def hand_over(q, k, v, curv, q_out, k_out, v_out, curv_out, held, read, written):
    batch = q.shape[0]
    parts = [(number, b) for number in range(3) for b in range(batch)]
    sources, outs = (q, k, v), (q_out, k_out, v_out)
    reads, writes = [], []
    for number, b in parts:
        reads.append(
            pltpu.make_async_copy(sources[number].at[b], held.at[number, b], read.at[number, b])
        )
        writes.append(
            pltpu.make_async_copy(held.at[number, b], outs[number].at[b], written.at[number, b])
        )
    for copy in reads:
        copy.start()
    curv_out[...] = curv[...]
    for first, second in zip(reads, writes):
        first.wait()
        second.start()
    for copy in writes:
        copy.wait()


def local(n, m, queries, key_rows, value_rows, query_tangent, key_tangent, out_adjoint):
    batch, tokens, width = queries.shape
    local_heads = width // HEAD_DIM
    length = n * tokens
    heads = local_heads * m
    board_shape = (-(-batch // 8) * 8, -(-heads // 128) * 128)
    result = jax.ShapeDtypeStruct(queries.shape, BF16)
    D = HEAD_DIM
    landed = pl.pallas_call(
        functools.partial(kernel, n, m, local_heads),
        out_shape=(result, result, result, jax.ShapeDtypeStruct((batch, heads), F32)),
        in_specs=[pl.BlockSpec(memory_space=pl.ANY)] * 6,
        out_specs=(pl.BlockSpec(memory_space=pltpu.VMEM),) * 4,
        scratch_shapes=[
            pltpu.VMEM((SLOTS * length // 2, 2 * D), BF16),
            pltpu.VMEM((SLOTS * length, 2 * D), BF16),
            pltpu.VMEM((SLOTS * length // 2, D), BF16),
            pltpu.VMEM((SLOTS * length, D), BF16),
            pltpu.VMEM((3 * length, D), BF16),
            pltpu.VMEM((length, D), F32),
            pltpu.VMEM((length, D), F32),
            pltpu.VMEM((SLOTS * length // 2, D), BF16),
            pltpu.VMEM((SLOTS * length, D), BF16),
            pltpu.VMEM((SLOTS * length, D), BF16),
            pltpu.VMEM(queries.shape, BF16),
            pltpu.VMEM(queries.shape, BF16),
            pltpu.VMEM(board_shape, F32),
            pltpu.VMEM((n * m,) + board_shape, F32),
            pltpu.SemaphoreType.DMA((6,)),
            pltpu.SemaphoreType.DMA((SLOTS, 6)),
            pltpu.SemaphoreType.DMA((4,)),
            pltpu.SemaphoreType.DMA((3,)),
            pltpu.SemaphoreType.DMA((3,)),
            pltpu.SemaphoreType.DMA((2,)),
            pltpu.SemaphoreType.DMA,
            pltpu.SemaphoreType.DMA,
        ],
        compiler_params=pltpu.CompilerParams(
            collective_id=0, has_side_effects=True, vmem_limit_bytes=56 * 1024 * 1024
        ),
    )(queries, key_rows, value_rows, query_tangent, key_tangent, out_adjoint)
    return pl.pallas_call(
        hand_over,
        out_shape=(result, result, result, jax.ShapeDtypeStruct((batch, heads), F32)),
        in_specs=[pl.BlockSpec(memory_space=pl.ANY)] * 3 + [pl.BlockSpec(memory_space=pltpu.VMEM)],
        out_specs=(
            pl.BlockSpec(memory_space=pl.ANY),
            pl.BlockSpec(memory_space=pl.ANY),
            pl.BlockSpec(memory_space=pl.ANY),
            pl.BlockSpec(memory_space=pltpu.VMEM),
        ),
        scratch_shapes=[
            pltpu.VMEM((3,) + queries.shape, BF16),
            pltpu.SemaphoreType.DMA((3, batch)),
            pltpu.SemaphoreType.DMA((3, batch)),
        ],
    )(*landed)


def solution(mesh):
    split = P(None, "seq", "dp")
    return jax.shard_map(
        functools.partial(local, mesh.shape["seq"], mesh.shape["dp"]),
        mesh=mesh,
        in_specs=(split,) * 6,
        out_specs=(split, split, split, P()),
        check_vma=False,
    )
```

```python
import functools
import math

import jax
import jax.numpy as jnp
from jax import lax
from jax.experimental import pallas as pl
from jax.experimental.pallas import tpu as pltpu
from jax.sharding import PartitionSpec as P

HEAD_DIM = 128
ROWS = 256
SLOTS = 3
MESH = pl.DeviceIdType.MESH
F32 = jnp.float32
BF16 = jnp.bfloat16


def mm(left, right, dims):
    return lax.dot_general(left, right, (dims, ((), ())), preferred_element_type=F32)


def kernel(
    n,
    m,
    local_heads,
    q_in,
    k_in,
    v_in,
    tq_in,
    tk_in,
    g_in,
    q_out,
    k_out,
    v_out,
    curv_out,
    qq,
    kk,
    gg,
    vv,
    hk_acc,
    hv_acc,
    q_staged,
    k_staged,
    v_staged,
    k_low,
    v_low,
    mine,
    board,
    in_send,
    in_recv,
    out_send,
    out_recv,
    low_recv,
    board_send,
    board_recv,
):
    D = HEAD_DIM
    me = lax.axis_index("seq")
    dp = lax.axis_index("dp")
    tokens = q_in.shape[1]
    quarter = n // 4
    half = n // 2
    length = n * tokens
    upper = half * tokens
    rows = min(ROWS, upper)
    per_block = rows // tokens
    factor = D ** (-0.5)
    level = me // quarter
    ring = me % quarter
    near = 1 - level % 2
    low = level < 2
    slots = 1 + (SLOTS - 1) * near

    barrier = pltpu.get_barrier_semaphore()

    def greet(step, carry):
        other = lax.rem(dp * n + me + step, n * m)
        pl.semaphore_signal(
            barrier, inc=1, device_id=(other % n, other // n), device_id_type=MESH
        )
        return carry

    lax.fori_loop(1, n * m, greet, 0)

    tensors = (
        (k_in, kk, 0, length),
        (tk_in, kk, D, length),
        (v_in, vv, 0, length),
        (q_in, qq, D, upper),
        (tq_in, qq, 0, upper),
        (g_in, gg, 0, upper),
    )

    def columns(pair):
        return pl.ds(pl.multiple_of((pair % local_heads) * D, D), D)

    def feed(number, pair, slot, home, row):
        source, buf, column, span = tensors[number]
        src = source.at[pair // local_heads, :, columns(pair)]
        at = pl.multiple_of(slot * span + row, tokens)
        dst = buf.at[pl.ds(at, tokens), column : column + D]

        @pl.when(home == me)
        def _():
            pltpu.make_async_copy(src, dst, in_recv.at[slot, number]).start()

        @pl.when(home != me)
        def _():
            pltpu.make_async_remote_copy(
                src_ref=src,
                dst_ref=dst,
                send_sem=in_send.at[number],
                recv_sem=in_recv.at[slot, number],
                device_id=(home, dp),
                device_id_type=MESH,
            ).start()

    pl.semaphore_wait(barrier, n * m - 1)

    for group in (0, 3, 1, 2):
        far = 1 if group == 3 else 0
        slot = 0 if far else group

        def send(step, carry, group=group, far=far, slot=slot):
            spot = (me + step) % quarter
            pair = group * quarter + spot
            low_home = far * quarter + spot
            high_home = half + far * quarter + spot

            @pl.when(low)
            def _():
                for number in range(6):
                    feed(number, pair, slot, low_home, me * tokens)
                for number in range(3):
                    feed(number, pair, slot, high_home, me * tokens)

            @pl.when(jnp.logical_not(low))
            def _():
                for number in range(3):
                    feed(number, pair, slot, high_home, me * tokens)
                for number in range(3, 6):
                    feed(number, pair, slot, high_home, (me - half) * tokens)

            return carry

        lax.fori_loop(0, quarter, send, 0)

    shape = mine.shape
    mine[...] = jnp.zeros(shape, F32)

    def ship(staged, at, other, dst, number, recv):
        src = staged.at[pl.ds(pl.multiple_of(at, tokens), tokens), :]

        @pl.when(other == me)
        def _():
            pltpu.make_async_copy(src, dst, recv).start()

        @pl.when(other != me)
        def _():
            pltpu.make_async_remote_copy(
                src_ref=src,
                dst_ref=dst,
                send_sem=out_send.at[number],
                recv_sem=recv,
                device_id=(other, dp),
                device_id_type=MESH,
            ).start()

    def work(slot, base):
        group = near * slot + (1 - near) * 3
        pair = group * quarter + ring
        batch = pair // local_heads
        cols = columns(pair)
        keys = base + upper
        top_rows = pl.multiple_of(slot * upper, rows)
        top_keys = pl.multiple_of(slot * length, rows)

        def arrived(number, count):
            _, buf, column, span = tensors[number]
            whole = buf.at[:count, column : column + D]
            pltpu.make_async_copy(whole, whole, in_recv.at[slot, number]).wait()

        for number in range(6):
            arrived(number, keys if number < 3 else upper)

        kappa = jnp.zeros((1, 1), F32)
        for start in reversed(range(base, keys, rows)):
            width = start + rows
            here = pl.ds(pl.multiple_of(top_rows + (start - base), rows), rows)
            seen = pl.ds(top_keys, width)
            both = qq[here, :]
            adj = gg[here, :]
            both_keys = kk[seen, :]
            scores = mm(both[:, D:], both_keys[:, :D], ((1,), (1,)))
            row = lax.broadcasted_iota(jnp.int32, (rows, width), 0) + start
            col = lax.broadcasted_iota(jnp.int32, (rows, width), 1)
            scores = jnp.where(row >= col, scores, -jnp.inf)
            top = jnp.max(scores, axis=1, keepdims=True)
            weights = jnp.exp2((scores - top) * (factor * math.log2(math.e)))
            probs = weights * (1.0 / jnp.sum(weights, axis=1, keepdims=True))
            tangent = factor * mm(both, both_keys, ((1,), (1,)))
            mean = jnp.sum(probs * tangent, axis=1, keepdims=True)
            tprobs = probs * (tangent - mean)
            gprobs = mm(adj, vv[seen, :], ((1,), (1,)))
            delta = jnp.sum(probs * gprobs, axis=1, keepdims=True)
            centered = gprobs - delta
            tdelta = jnp.sum(tprobs * gprobs, axis=1, keepdims=True)
            tprob_low = tprobs.astype(BF16)
            gscore_low = (probs * centered).astype(BF16)
            second_low = (tprobs * centered - probs * tdelta).astype(BF16)
            hv = mm(tprob_low, adj, ((0,), (0,)))
            hq = factor * (
                mm(second_low, both_keys[:, :D], ((1,), (0,)))
                + mm(gscore_low, both_keys[:, D:], ((1,), (0,)))
            )
            hk = factor * (
                mm(second_low, both[:, D:], ((0,), (0,)))
                + mm(gscore_low, both[:, :D], ((0,), (0,)))
            )
            if width == keys:
                hk_acc[:keys, :] = hk
                hv_acc[:keys, :] = hv
            else:
                hk_acc[:width, :] += hk
                hv_acc[:width, :] += hv
            kappa += jnp.sum(both[:, :D].astype(F32) * hq, keepdims=True)
            q_staged[here, :] = hq.astype(BF16)

            done = start if start > base else 0
            count = width - done
            span = slice(done, width)
            area = pl.ds(pl.multiple_of(top_keys + done, rows), count)
            hk_done = hk_acc[span, :]
            kappa += jnp.sum(kk[area, D:].astype(F32) * hk_done, keepdims=True)
            k_staged[area, :] = hk_done.astype(BF16)
            v_staged[area, :] = hv_acc[span, :].astype(BF16)

            def give_q(step, carry, start=start):
                other = start // tokens + step
                at = top_rows + other * tokens - base
                ship(q_staged, at, other, q_out.at[batch, :, cols], 0, out_recv.at[0])
                return carry

            def give_kv(step, carry, done=done):
                other = done // tokens + step
                at = top_keys + other * tokens
                if base:
                    ship(k_staged, at, other, k_out.at[batch, :, cols], 1, out_recv.at[1])
                    ship(v_staged, at, other, v_out.at[batch, :, cols], 2, out_recv.at[2])
                else:
                    ship(k_staged, at, other, k_low.at[batch, :, cols], 1, low_recv.at[0])
                    ship(v_staged, at, other, v_low.at[batch, :, cols], 2, low_recv.at[1])
                return carry

            lax.fori_loop(0, count // tokens, give_kv, 0)
            lax.fori_loop(0, per_block, give_q, 0)

        at_row = lax.broadcasted_iota(jnp.int32, shape, 0) == batch
        at_col = (
            lax.broadcasted_iota(jnp.int32, shape, 1) == dp * local_heads + pair % local_heads
        )
        mine[...] += jnp.where(jnp.logical_and(at_row, at_col), kappa, 0.0)

    def all_slots(base):
        def one(slot, carry):
            work(slot, base)
            return carry

        lax.fori_loop(0, slots, one, 0)

    @pl.when(low)
    def _():
        all_slots(0)

    @pl.when(jnp.logical_not(low))
    def _():
        all_slots(upper)

    place = dp * n + me

    def tell(step, carry):
        other = (place + step) % (n * m)
        pltpu.make_async_remote_copy(
            src_ref=mine,
            dst_ref=board.at[place],
            send_sem=board_send,
            recv_sem=board_recv,
            device_id=(other % n, other // n),
            device_id_type=MESH,
        ).start()
        return carry

    pltpu.make_async_copy(mine, board.at[place], board_recv).start()
    lax.fori_loop(1, n * m, tell, 0)

    def gone(units, sem):
        sent = vv.at[: units * tokens, :]
        pltpu.make_async_copy(sent, sent, sem).wait()

    for is_low in (True, False):
        for count, is_near in ((SLOTS, 1), (1, 0)):

            @pl.when(jnp.logical_and(low == is_low, near == is_near))
            def _(is_low=is_low, count=count):
                for number in range(6):
                    gone(n - count + (n if is_low and number < 3 else 0), in_send.at[number])
                gone(count * (half - 1), out_send.at[0])
                for number in (1, 2):
                    gone(count * ((half if is_low else n) - 1), out_send.at[number])

    sent = board.at[: n * m - 1]
    pltpu.make_async_copy(sent, sent, board_send).wait()

    pltpu.make_async_copy(q_out, q_out, out_recv.at[0]).wait()
    pltpu.make_async_copy(k_out, k_out, out_recv.at[1]).wait()
    pltpu.make_async_copy(v_out, v_out, out_recv.at[2]).wait()

    @pl.when(low)
    def _():
        pltpu.make_async_copy(k_low, k_low, low_recv.at[0]).wait()
        pltpu.make_async_copy(v_low, v_low, low_recv.at[1]).wait()
        k_out[...] = (k_out[...].astype(F32) + k_low[...].astype(F32)).astype(BF16)
        v_out[...] = (v_out[...].astype(F32) + v_low[...].astype(F32)).astype(BF16)

    pltpu.make_async_copy(board, board, board_recv).wait()
    total = jnp.sum(board[...], axis=0)
    curv_out[...] = total[: curv_out.shape[0], : curv_out.shape[1]]


def local(n, m, queries, key_rows, value_rows, query_tangent, key_tangent, out_adjoint):
    batch, tokens, width = queries.shape
    local_heads = width // HEAD_DIM
    length = n * tokens
    heads = local_heads * m
    board_shape = (-(-batch // 8) * 8, -(-heads // 128) * 128)
    result = jax.ShapeDtypeStruct(queries.shape, BF16)
    D = HEAD_DIM
    return pl.pallas_call(
        functools.partial(kernel, n, m, local_heads),
        out_shape=(result, result, result, jax.ShapeDtypeStruct((batch, heads), F32)),
        in_specs=[pl.BlockSpec(memory_space=pl.ANY)] * 6,
        out_specs=(pl.BlockSpec(memory_space=pltpu.VMEM),) * 4,
        scratch_shapes=[
            pltpu.VMEM((SLOTS * length // 2, 2 * D), BF16),
            pltpu.VMEM((SLOTS * length, 2 * D), BF16),
            pltpu.VMEM((SLOTS * length // 2, D), BF16),
            pltpu.VMEM((SLOTS * length, D), BF16),
            pltpu.VMEM((length, D), F32),
            pltpu.VMEM((length, D), F32),
            pltpu.VMEM((SLOTS * length // 2, D), BF16),
            pltpu.VMEM((SLOTS * length, D), BF16),
            pltpu.VMEM((SLOTS * length, D), BF16),
            pltpu.VMEM(queries.shape, BF16),
            pltpu.VMEM(queries.shape, BF16),
            pltpu.VMEM(board_shape, F32),
            pltpu.VMEM((n * m,) + board_shape, F32),
            pltpu.SemaphoreType.DMA((6,)),
            pltpu.SemaphoreType.DMA((SLOTS, 6)),
            pltpu.SemaphoreType.DMA((3,)),
            pltpu.SemaphoreType.DMA((3,)),
            pltpu.SemaphoreType.DMA((2,)),
            pltpu.SemaphoreType.DMA,
            pltpu.SemaphoreType.DMA,
        ],
        compiler_params=pltpu.CompilerParams(
            collective_id=0, has_side_effects=True, vmem_limit_bytes=56 * 1024 * 1024
        ),
    )(queries, key_rows, value_rows, query_tangent, key_tangent, out_adjoint)


def solution(mesh):
    split = P(None, "seq", "dp")
    return jax.shard_map(
        functools.partial(local, mesh.shape["seq"], mesh.shape["dp"]),
        mesh=mesh,
        in_specs=(split,) * 6,
        out_specs=(split, split, split, P()),
        check_vma=False,
    )
```
